32 devices in a mesh: dp: 4 (over y, core), expert: 8 (over z, x).
Axes of the slice: x: 2, y: 2, z: 4, core: 2. Of those that a mesh axis runs over, the one named last changes fastest.
Arguments:
- tokens_in: bfloat16 [32768, 768], P(('dp', 'expert')), may hold values from -6 to 6
- token_ids: int32 [32768], P(('dp', 'expert')), may hold values from 0 to 50303, as said below
- hash_table: int32 [50304], replicated, may hold values from 0 to 7, as said below
- gain_attn: bfloat16 [768], P(('dp', 'expert')), may hold values from 0.25 to 1.75
- gain_ffn: bfloat16 [768], P(('dp', 'expert')), may hold values from 0.25 to 1.75
- w_qkv: bfloat16 [768, 2304], P(('dp', 'expert')), may hold values from -0.21875 to 0.21875
- w_o: bfloat16 [768, 768], P(('dp', 'expert')), may hold values from -1.5 to 1.5
- w_in: bfloat16 [8, 768, 3072], P('expert', None, 'dp'), may hold values from -0.21875 to 0.21875
- w_out: bfloat16 [8, 3072, 768], P('expert', 'dp'), may hold values from -0.109375 to 0.109375
- cotangent: bfloat16 [32768, 768], P(('dp', 'expert')), may hold values from -6 to 6
Outputs:
- block_out: bfloat16 [32768, 768], P(('dp', 'expert'))
- grad_tokens: bfloat16 [32768, 768], P(('dp', 'expert'))
- grad_w_qkv: float32 [768, 2304], P(('dp', 'expert'))
- grad_w_o: float32 [768, 768], P(('dp', 'expert'))
- grad_gain_attn: float32 [768], P(('dp', 'expert'))
- grad_gain_ffn: float32 [768], P(('dp', 'expert'))
- grad_w_in: float32 [8, 768, 3072], P('expert', None, 'dp')
- grad_w_out: float32 [8, 3072, 768], P('expert', 'dp')
The draws below stay inside these ranges and needn't reach their ends.
Inputs may be any that keep to these rules, and one draw needn't show every extreme that they name: `hash_table`: each of the 8 experts is the value for exactly 6288 ids. `token_ids`: each aligned block of 1024 tokens holds at most 256 tokens that hash_table sends to any one expert, and exactly 256 for one expert, which is the same expert for all blocks of an aligned run of 8192 tokens.
All inputs are finite; a program needn't handle non-finite values.
Results may differ from the reference program's by a relative error of at most 0.013.
Values may be sent and summed in bfloat16 or wider, within the bound.
A program may use at most 256 MiB of HBM per device.

```python
import math
import jax
import jax.numpy as jnp
from jax import lax

D = 768
HEADS = 12
HDIM = 64
FF = 3072
VOCAB = 50304
TOK_DEV = 1024
SEQ = 1024
EXPERTS = 8
GROUPS = 4
TOKENS = 32768
MOST = 256


def mix_table(key):
    return jax.random.permutation(jax.random.fold_in(key, 7001), VOCAB).astype(jnp.int32)


def draw_hash_table(key, part):
    return (mix_table(key) % EXPERTS).astype(jnp.int32)


def draw_token_ids(key, part):
    mixed = mix_table(key)
    inverse = jnp.zeros((VOCAB,), jnp.int32).at[mixed].set(jnp.arange(VOCAB, dtype=jnp.int32))
    own_key = jax.random.fold_in(key, 7002)
    hot_key, spread_key, order_key, pick_key = jax.random.split(own_key, 4)
    device_count = GROUPS * EXPERTS
    hottest = jax.random.randint(hot_key, (GROUPS,), 0, EXPERTS).astype(jnp.int32)
    hot_device = jnp.repeat(hottest, EXPERTS)
    spread_keys = jax.random.split(spread_key, device_count)

    def place_others(one_key):
        return (jax.random.permutation(one_key, (EXPERTS - 1) * MOST)[:TOK_DEV - MOST] // MOST).astype(jnp.int32)
    places = jax.vmap(place_others)(spread_keys)
    others = (hot_device[:, None] + 1 + places) % EXPERTS
    owners = jnp.concatenate([jnp.broadcast_to(hot_device[:, None], (device_count, MOST)), others], axis=1)
    order_keys = jax.random.split(order_key, device_count)

    def reorder(one_key, owner_line):
        return owner_line[jax.random.permutation(one_key, TOK_DEV)]
    owners = jax.vmap(reorder)(order_keys, owners)
    within = jax.random.randint(pick_key, (device_count, TOK_DEV), 0, VOCAB // EXPERTS).astype(jnp.int32)
    token_list = inverse[within * EXPERTS + owners]
    return token_list.reshape(TOKENS).astype(jnp.int32)


def raised(values, rng, source, target, shards_of, factor):
    owner, partner = [(jnp.arange(values.shape[axis_at]) // (values.shape[axis_at] // shards_of)).reshape([-1 if axis == axis_at else 1 for axis in range(values.ndim)]) for axis_at in (source, target)]
    chosen = jax.random.permutation(rng, shards_of)[partner]
    strong = (owner == chosen) | (owner == (partner + shards_of // 2) % shards_of)
    return jnp.where(strong, factor * values, values)


def level_of(key, shape, shards, low, high):
    factor_of = 1.0
    for dim, shards_of in shards:
        draws = jax.random.uniform(jax.random.fold_in(jax.random.fold_in(key, 6), dim), (shards_of,), jnp.float32, low / len(shards), high / len(shards))
        factor_of = factor_of * jnp.repeat(jnp.exp(draws), shape[dim] // shards_of).reshape((-1,) + (1,) * (len(shape) - 1 - dim))
    return factor_of


def bell_draw(stream_key, extent, scale, most, pieces=(), kind=jnp.bfloat16):
    drawn = scale * jax.random.normal(stream_key, extent, jnp.float32)
    if pieces:
        drawn = drawn * level_of(stream_key, extent, pieces, -0.22, 0.18)
    return jnp.clip(drawn, -most, most).astype(kind)


def noise_with(key, extent, deviation, reach, cuts, heavy, kind=jnp.bfloat16):
    array = deviation * jax.random.normal(key, extent, jnp.float32)
    if cuts:
        array = array * level_of(key, extent, cuts, -0.22, 0.18)
    return jnp.clip(raised(array, jax.random.fold_in(key, 3), *heavy), -reach, reach).astype(kind)


def setup_inputs(seed: int = 0) -> dict:
    arg_keys = jax.random.split(jax.random.key(seed), 11)
    return {
        "tokens_in": noise_with(arg_keys[0], (TOKENS, D), 1.0, 6.0, ((0, 32),), (0, 1, 32, 2.75)),
        "token_ids": draw_token_ids(jax.random.fold_in(arg_keys[10], 71), 0),
        "hash_table": draw_hash_table(jax.random.fold_in(arg_keys[10], 71), 0),
        "gain_attn": jnp.clip(1.0 + 0.15 * jax.random.normal(arg_keys[3], (D,), jnp.float32), 0.25, 1.75).astype(jnp.bfloat16),
        "gain_ffn": jnp.clip(1.0 + 0.15 * jax.random.normal(arg_keys[4], (D,), jnp.float32), 0.25, 1.75).astype(jnp.bfloat16),
        "w_qkv": bell_draw(arg_keys[5], (D, 3 * D), D ** -0.5, 0.21875, ((0, 32),)),
        "w_o": bell_draw(arg_keys[6], (D, D), (D // 48) ** -0.5, 1.5, ((0, 32),)),
        "w_in": bell_draw(arg_keys[7], (EXPERTS, D, FF), D ** -0.5, 0.21875, ((0, 8), (2, 4))),
        "w_out": bell_draw(arg_keys[8], (EXPERTS, FF, D), FF ** -0.5, 0.109375, ((0, 8), (1, 4))),
        "cotangent": bell_draw(arg_keys[9], (TOKENS, D), 1.0, 6.0, ((0, 32),)),
    }


@jax.custom_vjp
def low(v):
    return lax.optimization_barrier(v.astype(jnp.bfloat16)).astype(jnp.float32)

@jax.custom_vjp
def low_back(v):
    return v

def low_keep(v):
    return (low(v), None)

def low_pass(kept, grad):
    return (grad,)

def back_keep(v):
    return (v, None)

def back_low(kept, grad):
    return (low(grad),)
low.defvjp(low_keep, low_pass)
low_back.defvjp(back_keep, back_low)
EPS = 1e-05
HIGH = lax.Precision.HIGHEST
NEG = -1e+30
GELU_C = 0.7978845608028654

def gelu_tanh(values):
    return 0.5 * values * (1.0 + jnp.tanh(GELU_C * (values + 0.044715 * values * values * values)))

def norm_rows(values, gain):
    centre = lax.optimization_barrier(jnp.mean(values, axis=-1, keepdims=True))
    shifted = values - centre
    spread = lax.optimization_barrier(jnp.mean(shifted * shifted, axis=-1, keepdims=True))
    return shifted * lax.rsqrt(spread + EPS) * gain

def attend(block_in, gain_attn, w_qkv, w_o):
    seq_count = block_in.shape[0]
    act_one = low(norm_rows(block_in, gain_attn))
    qkv = low(low_back(jnp.einsum('gtd,de->gte', act_one, w_qkv, precision=HIGH)))
    query_rows = qkv[..., :D].reshape(seq_count, SEQ, HEADS, HDIM)
    key_rows = qkv[..., D:2 * D].reshape(seq_count, SEQ, HEADS, HDIM)
    value_rows = qkv[..., 2 * D:].reshape(seq_count, SEQ, HEADS, HDIM)
    scores = jnp.einsum('gqhd,gkhd->ghqk', query_rows, key_rows, precision=HIGH) * HDIM ** (-0.5)
    scores = low_back(scores)
    causal = jnp.arange(SEQ, dtype=jnp.int32)[:, None] >= jnp.arange(SEQ, dtype=jnp.int32)[None, :]
    scores = jnp.where(causal[None, None], scores, NEG)
    probs = low(jax.nn.softmax(scores, axis=-1))
    context = jnp.einsum('ghqk,gkhd->gqhd', probs, value_rows, precision=HIGH).reshape(seq_count, SEQ, D)
    context = low(low_back(context))
    return block_in + low_back(jnp.einsum('gtd,de->gte', context, w_o, precision=HIGH))

def expert_run(expert_args):
    rows_in, weight_in, weight_out = expert_args
    pre_act = low_back(jnp.dot(rows_in, weight_in, precision=HIGH))
    hidden = low(gelu_tanh(pre_act))
    return low(low_back(jnp.dot(hidden, weight_out, precision=HIGH)))

def forward(tokens_in, gain_attn, gain_ffn, w_qkv, w_o, w_in, w_out, slot_index, source_rows, valid_rows):
    seq_total = TOKENS // SEQ
    together = math.gcd(seq_total, max(1, 4096 // SEQ))
    seq_blocks = tokens_in.reshape(seq_total // together, together, SEQ, D)

    def attend_block(seq_block):
        return attend(seq_block, gain_attn, w_qkv, w_o)
    mixed = lax.map(jax.checkpoint(attend_block), seq_blocks).reshape(TOKENS, D)
    act_two = low(low_back(norm_rows(mixed, gain_ffn)))
    capacity = GROUPS * EXPERTS * MOST

    def expert_step(total, expert_args):
        row_ids, row_valid, weight_in, weight_out = expert_args
        rows_in = act_two[row_ids] * row_valid[:, None]
        result = expert_run((rows_in, weight_in, weight_out)) * row_valid[:, None]
        return (total.at[row_ids].add(result), None)
    start = jnp.zeros((TOKENS, D), mixed.dtype)
    expert_out, _ = lax.scan(jax.checkpoint(expert_step), start, (source_rows.reshape(EXPERTS, capacity), valid_rows.reshape(EXPERTS, capacity), w_in, w_out))
    return mixed + expert_out

def reference(tokens_in, token_ids, hash_table, gain_attn, gain_ffn, w_qkv, w_o, w_in, w_out, cotangent):
    capacity = GROUPS * EXPERTS * MOST
    expert_ids = hash_table[token_ids].astype(jnp.int32)
    one_hot = (expert_ids[:, None] == jnp.arange(EXPERTS, dtype=jnp.int32)[None, :]).astype(jnp.int32)
    before = jnp.cumsum(one_hot, axis=0) - one_hot
    slot_index = (expert_ids * capacity + lax.optimization_barrier(jnp.sum(before * one_hot, axis=1))).astype(jnp.int32)
    source_rows = jnp.zeros((EXPERTS * capacity,), jnp.int32).at[slot_index].set(jnp.arange(TOKENS, dtype=jnp.int32))
    valid_rows = jnp.zeros((EXPERTS * capacity,), jnp.float32).at[slot_index].set(1.0)
    float_args = tuple((array_in.astype(jnp.float32) for array_in in (tokens_in, gain_attn, gain_ffn, w_qkv, w_o, w_in, w_out)))

    def forward_floats(tok_f, gain_a, gain_f, qkv_f, out_f, in_f, expert_f):
        return forward(tok_f, gain_a, gain_f, qkv_f, out_f, in_f, expert_f, slot_index, source_rows, valid_rows.astype(tok_f.dtype))
    block_out, pullback = jax.vjp(forward_floats, *float_args)
    grads = pullback(cotangent.astype(jnp.float32))
    grad_tokens, grad_gain_attn, grad_gain_ffn, grad_w_qkv, grad_w_o, grad_w_in, grad_w_out = grads
    return (block_out.astype(jnp.bfloat16), grad_tokens.astype(jnp.bfloat16), grad_w_qkv, grad_w_o, grad_gain_attn, grad_gain_ffn, grad_w_in, grad_w_out)
```

```python
import jax
import jax.numpy as jnp
from jax import lax
from jax.experimental import pallas as pl
from jax.experimental.pallas import tpu as pltpu
from jax.sharding import PartitionSpec as P

HEADS = 12
SEQ = 1024


EPS = 1e-05
NEG = -1e30
GELU_C = 0.7978845608028654


def gelu_tanh(values):
    return 0.5 * values * (1.0 + jnp.tanh(GELU_C * (values + 0.044715 * values * values * values)))


def gelu_slope(values):
    inner = jnp.tanh(GELU_C * (values + 0.044715 * values * values * values))
    return 0.5 * (1.0 + inner) + 0.5 * values * (1.0 - inner * inner) * GELU_C * (
        1.0 + 3.0 * 0.044715 * values * values
    )


def norm_parts(values):
    centre = jnp.mean(values, axis=-1, keepdims=True)
    shifted = values - centre
    spread = jnp.mean(shifted * shifted, axis=-1, keepdims=True)
    inverse = lax.rsqrt(spread + EPS)
    return (shifted * inverse, inverse)


def norm_grad(upstream, gain, normed, inverse):
    scaled = upstream * gain
    return inverse * (
        scaled
        - jnp.mean(scaled, axis=-1, keepdims=True)
        - normed * jnp.mean(scaled * normed, axis=-1, keepdims=True)
    )


def contract_rows(left, right):
    return lax.dot_general(
        left, right, (((0,), (0,)), ((), ())), preferred_element_type=jnp.float32
    )


def contract_cols(left, right):
    return lax.dot_general(
        left, right, (((1,), (1,)), ((), ())), preferred_element_type=jnp.float32
    )


F32 = jnp.float32
BF = jnp.bfloat16
QB = 256
def dot(a,b): return jnp.dot(a,b,preferred_element_type=F32)
def dot_nt(a,b): return lax.dot_general(a,b,(((1,),(1,)),((),())),preferred_element_type=F32)

def head_masks():
    lane = lax.broadcasted_iota(jnp.int32,(1,128),1)
    lo = jnp.where(lane<64,1.0,0.0)
    return [lo.astype(BF),(1.0-lo).astype(BF)]

def attn_fwd_pair(p, seq, width, qkv_ref, ctx_ref, lse_ref):
    off = pl.multiple_of(p*128,128)
    masks = head_masks()
    lane_lo = lax.broadcasted_iota(jnp.int32,(QB,128),1)<64
    nb = seq//QB
    kp = qkv_ref[:, pl.ds(pl.multiple_of(width+off,128),128)]
    vp = qkv_ref[:, pl.ds(pl.multiple_of(2*width+off,128),128)]
    vts = [(vp*m+(1-m)).T for m in masks]
    causal = lax.broadcasted_iota(jnp.int32,(QB,QB),0)<=lax.broadcasted_iota(jnp.int32,(QB,QB),1)
    for i in range(nb):
        nk=(i+1)*QB
        qb = qkv_ref[pl.ds(i*QB,QB), pl.ds(off,128)]
        outs=[]
        for hh in range(2):
            qh = qb*(masks[hh]*0.125).astype(BF)
            st = dot_nt(kp[:nk], qh)
            diag = jnp.where(causal, st[nk-QB:], -1e30)
            m = jnp.max(diag,axis=0,keepdims=True)
            if i:
                m = jnp.maximum(m, jnp.max(st[:nk-QB],axis=0,keepdims=True))
            pd = jnp.exp(diag-m).astype(BF)
            ot = dot(vts[hh][:, nk-QB:nk], pd)
            if i:
                po = jnp.exp(st[:nk-QB]-m).astype(BF)
                ot = ot + dot(vts[hh][:, :nk-QB], po)
            l = ot[64:65] if hh==0 else ot[0:1]
            outs.append((ot*(1.0/l)))
            lse_ref[pl.ds(2*p+hh,1), pl.ds(i*QB,QB)] = m+jnp.log(l)
        sub_lo = lax.broadcasted_iota(jnp.int32,(128,QB),0)<64
        o = jnp.where(sub_lo, outs[0], outs[1]).T
        ctx_ref[pl.ds(i*QB,QB), pl.ds(off,128)] = o.astype(BF)

def attn_bwd_pair(p, seq, width, qkv_ref, ctx_ref, lse_ref, do_ref, dqkv_ref, dqt_ref):
    off = pl.multiple_of(p*128,128)
    masks = head_masks()
    nb = seq//QB
    koff = pl.multiple_of(width+off,128); voff=pl.multiple_of(2*width+off,128)
    qp = qkv_ref[:, pl.ds(off,128)]
    kp = qkv_ref[:, pl.ds(koff,128)]
    dop = do_ref[:, pl.ds(off,128)]
    prod = dop.astype(F32)*ctx_ref[:, pl.ds(off,128)].astype(F32)
    sel = (lax.broadcasted_iota(jnp.int32,(8,128),1)//64 == lax.broadcasted_iota(jnp.int32,(8,128),0)).astype(F32)
    delta = lax.dot_general(sel, prod, (((1,),(1,)),((),())), preferred_element_type=F32, precision=lax.Precision.HIGHEST)
    causal = lax.broadcasted_iota(jnp.int32,(QB,QB),0)<=lax.broadcasted_iota(jnp.int32,(QB,QB),1)
    qs = [qp*(m*0.125).astype(BF) for m in masks]
    dos = [dop*m for m in masks]
    kts = [(kp*(m*0.125).astype(BF)).T for m in masks]
    lses = [lse_ref[pl.ds(2*p+hh,1), :] for hh in range(2)]
    for j in range(nb):
        q0=j*QB
        kj = qkv_ref[pl.ds(q0,QB), pl.ds(koff,128)]
        vj = qkv_ref[pl.ds(q0,QB), pl.ds(voff,128)]
        dk=None; dv=None; dq=None
        for hh in range(2):
            st = dot_nt(kj, qs[hh][q0:])
            pt = jnp.exp(st-lses[hh][:, q0:])
            dpt = dot_nt(vj, dos[hh][q0:])
            if nb-j>1:
                pt = jnp.concatenate([jnp.where(causal, pt[:, :QB], 0.0), pt[:, QB:]],axis=1)
            else:
                pt = jnp.where(causal, pt, 0.0)
            dst = (pt*(dpt-delta[hh:hh+1, q0:])).astype(BF)
            ptl = pt.astype(BF)
            a = dot(ptl, dos[hh][q0:]); b = dot(dst, qs[hh][q0:]); c = dot(kts[hh][:, q0:q0+QB], dst)
            dv = a if dv is None else dv+a
            dk = b if dk is None else dk+b
            dq = c if dq is None else dq+c
        dqkv_ref[pl.ds(q0,QB), pl.ds(koff,128)] = dk.astype(BF)
        dqkv_ref[pl.ds(q0,QB), pl.ds(voff,128)] = dv.astype(BF)
        if j==0:
            dqt_ref[...] = dq
        else:
            dqt_ref[:, pl.ds(q0,seq-q0)] += dq
    dqkv_ref[:, pl.ds(off,128)] = dqt_ref[...].T.astype(BF)

def fwd_kernel(act_ref, w_ref, qkv_ref, ctx_ref, lse_ref):
    seq,width = act_ref.shape
    @pl.loop(0, 3*width//256)
    def _(n):
        c = pl.ds(pl.multiple_of(n*256,256),256)
        qkv_ref[:, c] = dot(act_ref[...], w_ref[:, c]).astype(BF)
    @pl.loop(0, width//128)
    def _(p):
        attn_fwd_pair(p, seq, width, qkv_ref, ctx_ref, lse_ref)

def bwd_kernel(qkv_ref, ctx_ref, lse_ref, do_ref, dqkv_ref, dqt_ref):
    seq,width = ctx_ref.shape
    @pl.loop(0, width//128)
    def _(p):
        attn_bwd_pair(p, seq, width, qkv_ref, ctx_ref, lse_ref, do_ref, dqkv_ref, dqt_ref)


VM = pl.BlockSpec(memory_space=pltpu.VMEM)


def attention_forward(act, w):
    seq, width = act.shape
    return pl.pallas_call(
        fwd_kernel,
        out_shape=(
            jax.ShapeDtypeStruct((seq, 3 * width), BF),
            jax.ShapeDtypeStruct((seq, width), BF),
            jax.ShapeDtypeStruct((16, seq), F32),
        ),
        in_specs=[VM] * 2,
        out_specs=(VM,) * 3,
        compiler_params=pltpu.CompilerParams(vmem_limit_bytes=56 << 20),
    )(act, w)


def attention_backward(qkv, ctx, lse, do):
    seq, width = ctx.shape
    return pl.pallas_call(
        bwd_kernel,
        out_shape=jax.ShapeDtypeStruct((seq, 3 * width), BF),
        in_specs=[VM] * 4,
        out_specs=VM,
        scratch_shapes=[pltpu.VMEM((128, seq), F32)],
        compiler_params=pltpu.CompilerParams(vmem_limit_bytes=56 << 20),
    )(qkv, ctx, lse, do)


def attention_weights(gain_attn, gain_ffn, w_qkv, w_o):
    axes = ("dp", "expert")
    width = w_o.shape[1]
    packed = jnp.concatenate([w_o, gain_attn[:, None], gain_ffn[:, None]], axis=1)
    qkv_full = lax.all_gather(w_qkv, axes, axis=0, tiled=True)
    rest = lax.all_gather(packed, axes, axis=0, tiled=True)
    return qkv_full, rest[:, :width], rest[:, width], rest[:, width + 1]


def per_device(
    tokens_in, token_ids, hash_table, gain_attn, gain_ffn, w_qkv, w_o, w_in, w_out, cotangent
):
    tok_rows, model_width = tokens_in.shape
    n_expert = lax.axis_size("expert")
    slot_most = 2 * tok_rows // n_expert
    slot_count = n_expert * slot_most
    qkv_full, out_full, gain_one, gain_two = attention_weights(gain_attn, gain_ffn, w_qkv, w_o)
    gain_one = gain_one.astype(jnp.float32)
    gain_two = gain_two.astype(jnp.float32)
    inputs = tokens_in.astype(jnp.float32)
    normed_one, inverse_one = norm_parts(inputs)
    act_one = (normed_one * gain_one).astype(jnp.bfloat16)
    qkv, context, lse = attention_forward(act_one, qkv_full)
    mixed = inputs + jnp.dot(context, out_full, preferred_element_type=jnp.float32)
    normed_two, inverse_two = norm_parts(mixed)
    act_two = (normed_two * gain_two).astype(jnp.bfloat16)
    expert_ids = hash_table[token_ids]
    one_hot = (expert_ids[:, None] == jnp.arange(n_expert, dtype=jnp.int32)[None, :]).astype(
        jnp.int32
    )
    before = jnp.cumsum(one_hot, axis=0) - one_hot
    slot_index = expert_ids * slot_most + jnp.sum(before * one_hot, axis=1)
    send_rows = jnp.zeros((slot_count, model_width), jnp.bfloat16).at[slot_index].set(act_two)
    recv_rows = lax.all_to_all(
        send_rows.reshape(n_expert, slot_most, model_width),
        "expert",
        split_axis=0,
        concat_axis=0,
        tiled=True,
    ).reshape(slot_count, model_width)
    w_in_full, w_out_full = (
        lax.all_gather(w_in, "dp", axis=2, tiled=True),
        lax.all_gather(w_out, "dp", axis=1, tiled=True),
    )
    w_in_full = w_in_full[0]
    w_out_full = w_out_full[0]
    pre_act = jnp.dot(recv_rows, w_in_full, preferred_element_type=jnp.float32)
    hidden = gelu_tanh(pre_act).astype(jnp.bfloat16)
    expert_out = jnp.dot(hidden, w_out_full, preferred_element_type=jnp.float32).astype(
        jnp.bfloat16
    )
    returned = lax.all_to_all(
        expert_out.reshape(n_expert, slot_most, model_width),
        "expert",
        split_axis=0,
        concat_axis=0,
        tiled=True,
    ).reshape(slot_count, model_width)
    branch_out = returned[slot_index]
    block_out = (mixed + branch_out.astype(jnp.float32)).astype(jnp.bfloat16)
    grad_send = jnp.zeros((slot_count, model_width), jnp.bfloat16).at[slot_index].set(cotangent)
    grad_rows = lax.all_to_all(
        grad_send.reshape(n_expert, slot_most, model_width),
        "expert",
        split_axis=0,
        concat_axis=0,
        tiled=True,
    ).reshape(slot_count, model_width)
    grad_out_full = contract_rows(hidden, grad_rows)
    grad_hidden = contract_cols(grad_rows, w_out_full)
    grad_pre = (grad_hidden * gelu_slope(pre_act)).astype(jnp.bfloat16)
    grad_in_full = contract_rows(recv_rows, grad_pre)
    grad_act = contract_cols(grad_pre, w_in_full).astype(jnp.bfloat16)
    grad_w_in, grad_w_out = (
        lax.psum_scatter(
            grad_in_full[None].astype(jnp.bfloat16), "dp", scatter_dimension=2, tiled=True
        ).astype(jnp.float32),
        lax.psum_scatter(
            grad_out_full[None].astype(jnp.bfloat16), "dp", scatter_dimension=1, tiled=True
        ).astype(jnp.float32),
    )
    grad_back = lax.all_to_all(
        grad_act.reshape(n_expert, slot_most, model_width),
        "expert",
        split_axis=0,
        concat_axis=0,
        tiled=True,
    ).reshape(slot_count, model_width)
    grad_act_two = grad_back[slot_index].astype(jnp.float32)
    grad_gain_two = jnp.sum(grad_act_two * normed_two, axis=0)
    grad_mixed = cotangent.astype(jnp.float32) + norm_grad(
        grad_act_two, gain_two, normed_two, inverse_two
    )
    grad_branch = grad_mixed.astype(jnp.bfloat16)
    grad_out_proj = contract_rows(context, grad_branch)
    grad_context = contract_cols(grad_branch, out_full).astype(jnp.bfloat16)
    grad_qkv = attention_backward(qkv, context, lse, grad_context)
    grad_qkv_proj = contract_rows(act_one, grad_qkv)
    grad_act_one = contract_cols(grad_qkv, qkv_full)
    grad_gain_one = jnp.sum(grad_act_one * normed_one, axis=0)
    grad_tokens = (grad_mixed + norm_grad(grad_act_one, gain_one, normed_one, inverse_one)).astype(
        jnp.bfloat16
    )
    axes = ("dp", "expert")
    grad_w_qkv = lax.psum_scatter(
        grad_qkv_proj.astype(BF), axes, scatter_dimension=0, tiled=True
    ).astype(F32)
    grad_w_o = lax.psum_scatter(
        grad_out_proj.astype(BF), axes, scatter_dimension=0, tiled=True
    ).astype(F32)
    gains = lax.psum(jnp.stack([grad_gain_one, grad_gain_two]), axes)
    me = lax.axis_index("dp") * n_expert + lax.axis_index("expert")
    rows = gain_attn.shape[0]
    mine = lax.dynamic_slice(gains, (0, me * rows), (2, rows))
    grad_gain_attn, grad_gain_ffn = mine[0], mine[1]
    return (
        block_out,
        grad_tokens,
        grad_w_qkv,
        grad_w_o,
        grad_gain_attn,
        grad_gain_ffn,
        grad_w_in,
        grad_w_out,
    )


def solution(mesh):
    return jax.shard_map(
        per_device,
        mesh=mesh,
        in_specs=(
            P(("dp", "expert"), None),
            P(("dp", "expert")),
            P(),
            P(("dp", "expert")),
            P(("dp", "expert")),
            P(("dp", "expert"), None),
            P(("dp", "expert"), None),
            P("expert", None, "dp"),
            P("expert", "dp", None),
            P(("dp", "expert"), None),
        ),
        out_specs=(
            P(("dp", "expert"), None),
            P(("dp", "expert"), None),
            P(("dp", "expert"), None),
            P(("dp", "expert"), None),
            P(("dp", "expert")),
            P(("dp", "expert")),
            P("expert", None, "dp"),
            P("expert", "dp", None),
        ),
        check_vma=False,
    )
```
